32 devices in a mesh: dp: 4 (over y, x), ctx: 8 (over z, core).
Axes of the slice: x: 2, y: 2, z: 4, core: 2. Of those that a mesh axis runs over, the one named last changes fastest.
Arguments:
- inputs: bfloat16 [8, 512, 1536], P('dp', 'ctx'), may hold values from -6 to 6
- cotangent: bfloat16 [8, 512, 1536], P('dp', 'ctx'), may hold values from -6 to 6
- query_weight: bfloat16 [1536, 1536], P(('dp', 'ctx')), may hold values from -0.15625 to 0.15625
- key_weight: bfloat16 [1536, 768], P(('dp', 'ctx')), may hold values from -0.15625 to 0.15625
- value_weight: bfloat16 [1536, 768], P(('dp', 'ctx')), may hold values from -0.15625 to 0.15625
- output_weight: bfloat16 [1536, 1536], P(('dp', 'ctx')), may hold values from -2.5 to 2.5
- attn_gain: bfloat16 [1536], P(('dp', 'ctx')), may hold values from 0.25 to 1.75
- gate_weight: bfloat16 [1536, 4096], P(('dp', 'ctx')), may hold values from -0.15625 to 0.15625
- up_weight: bfloat16 [1536, 4096], P(('dp', 'ctx')), may hold values from -0.15625 to 0.15625
- down_weight: bfloat16 [4096, 1536], P(('dp', 'ctx')), may hold values from -0.09375 to 0.09375
- mlp_gain: bfloat16 [1536], P(('dp', 'ctx')), may hold values from 0.25 to 1.75
Outputs:
- layer_out: bfloat16 [8, 512, 1536], P('dp', 'ctx')
- inputs_grad: bfloat16 [8, 512, 1536], P('dp', 'ctx')
- query_grad: float32 [1536, 1536], P(('dp', 'ctx'))
- key_grad: float32 [1536, 768], P(('dp', 'ctx'))
- value_grad: float32 [1536, 768], P(('dp', 'ctx'))
- output_grad: float32 [1536, 1536], P(('dp', 'ctx'))
- attn_gain_grad: float32 [1536], P(('dp', 'ctx'))
- gate_grad: float32 [1536, 4096], P(('dp', 'ctx'))
- up_grad: float32 [1536, 4096], P(('dp', 'ctx'))
- down_grad: float32 [4096, 1536], P(('dp', 'ctx'))
- mlp_gain_grad: float32 [1536], P(('dp', 'ctx'))
The draws below stay inside these ranges and needn't reach their ends.
All inputs are finite; a program needn't handle non-finite values.
Results may differ from the reference program's by a relative error of at most 0.014.
Values may be sent and summed in bfloat16 or wider, within the bound.
No kernel may reach another device: no remote copies, remote signals or barrier semaphores. Data moves between devices by JAX's collectives and lax.ppermute only.
A program may use at most 320 MiB of HBM per device.

```python
import jax
import jax.numpy as jnp
from jax import lax

D = 1536
FF = 4096
HEADS = 16
KV_HEADS = 8
HEAD_DIM = 96
LENGTH = 512
SEQS = 8


def steps_of(stream_key, shape, pieces, smallest, largest):
    loudness, own = 1.0, jax.random.fold_in(stream_key, 6)
    for dim, blocks in pieces:
        draws = jnp.exp(jax.random.uniform(jax.random.fold_in(own, dim), (blocks,), jnp.float32, smallest / len(pieces), largest / len(pieces)))
        loudness = loudness * jnp.repeat(draws, shape[dim] // blocks).reshape([-1 if axis == dim else 1 for axis in range(len(shape))])
    return loudness


def gaussian(rng, shape, width, limit, shards=(), kind=jnp.bfloat16):
    entries = width * jax.random.normal(rng, shape, jnp.float32)
    if shards:
        entries = entries * steps_of(rng, shape, shards, -0.22, 0.18)
    return jnp.clip(entries, -limit, limit).astype(kind)


def setup_inputs(seed: int = 0) -> dict:
    seeds = jax.random.split(jax.random.key(seed), 12)
    inputs = gaussian(seeds[0], (SEQS, LENGTH, D), 1.0, 6.0, ((0, 4), (1, 8)))
    cotangent = gaussian(seeds[1], (SEQS, LENGTH, D), 1.0, 6.0, ((0, 4), (1, 8)))
    query_weight = gaussian(seeds[2], (D, HEADS * HEAD_DIM), D ** -0.5, 0.15625, ((0, 32),))
    key_weight = gaussian(seeds[3], (D, KV_HEADS * HEAD_DIM), D ** -0.5, 0.15625, ((0, 32),))
    value_weight = gaussian(seeds[4], (D, KV_HEADS * HEAD_DIM), D ** -0.5, 0.15625, ((0, 32),))
    output_weight = gaussian(seeds[5], (HEADS * HEAD_DIM, D), (max(1, 2 * D // LENGTH)) ** -0.5, 2.5, ((0, 32),))
    attn_gain = jnp.clip(1.0 + 0.15 * jax.random.normal(seeds[6], (D,), jnp.float32), 0.25, 1.75).astype(jnp.bfloat16)
    gate_weight = gaussian(seeds[7], (D, FF), D ** -0.5, 0.15625, ((0, 32),))
    up_weight = gaussian(seeds[8], (D, FF), D ** -0.5, 0.15625, ((0, 32),))
    down_weight = gaussian(seeds[9], (FF, D), FF ** -0.5, 0.09375, ((0, 32),))
    mlp_gain = jnp.clip(1.0 + 0.15 * jax.random.normal(seeds[10], (D,), jnp.float32), 0.25, 1.75).astype(jnp.bfloat16)
    return {"inputs": inputs, "cotangent": cotangent, "query_weight": query_weight, "key_weight": key_weight, "value_weight": value_weight, "output_weight": output_weight, "attn_gain": attn_gain, "gate_weight": gate_weight, "up_weight": up_weight, "down_weight": down_weight, "mlp_gain": mlp_gain}


epsilon = 1e-05
rope_base = 100000.0
highest = lax.Precision.HIGHEST

@jax.custom_vjp
def low(v):
    return lax.optimization_barrier(v.astype(jnp.bfloat16)).astype(jnp.float32)

@jax.custom_vjp
def low_back(v):
    return v

def low_keep(v):
    return (low(v), None)

def low_pass(kept, grad):
    return (grad,)

def back_keep(v):
    return (v, None)

def back_low(kept, grad):
    return (low(grad),)
low.defvjp(low_keep, low_pass)
low_back.defvjp(back_keep, back_low)

def product(left, right):
    return jnp.dot(left, right, preferred_element_type=jnp.float32, precision=highest)

def angles(row_count, start_pos, head_dim):
    half_dim = head_dim // 2
    positions = (start_pos + jnp.arange(row_count, dtype=jnp.int32)).astype(jnp.float32)
    frequency = rope_base ** (-(2.0 * jnp.arange(half_dim, dtype=jnp.float32)) / head_dim)
    angle_table = positions[:, None] * frequency[None, :]
    return (jnp.cos(angle_table), jnp.sin(angle_table))

def rotate(field, cosine, sine_table, head_dim):
    field_shape = field.shape
    split_heads = field.reshape(field_shape[:-1] + (field_shape[-1] // head_dim, head_dim))
    half_dim = head_dim // 2
    first_half = split_heads[..., :half_dim]
    second_half = split_heads[..., half_dim:]
    cos_part = cosine[:, None, :]
    sin_part = sine_table[:, None, :]
    rotated = jnp.concatenate([first_half * cos_part - second_half * sin_part, second_half * cos_part + first_half * sin_part], -1)
    return rotated.reshape(field_shape)

def attend(queries, keys_rot, values_low):
    seq_length = queries.shape[0]
    group_size = HEADS // KV_HEADS
    query_heads = queries.reshape(seq_length, KV_HEADS, group_size, HEAD_DIM).transpose(1, 0, 2, 3)
    key_heads = keys_rot.reshape(seq_length, KV_HEADS, HEAD_DIM).transpose(1, 0, 2)
    value_heads = values_low.reshape(seq_length, KV_HEADS, HEAD_DIM).transpose(1, 0, 2)
    positions = jnp.arange(seq_length, dtype=jnp.int32)
    allowed = positions[None, :] <= positions[:, None]

    def one_head(triple):
        query_portion, key_portion, value_portion = triple
        scores = low_back(jnp.einsum('cgd,ld->gcl', query_portion, key_portion, precision=highest))
        scores = jnp.where(allowed[None], scores, -1e+30)
        highest_score = lax.optimization_barrier(jnp.max(scores, -1, keepdims=True))
        log_total = highest_score + jnp.log(lax.optimization_barrier(jnp.sum(jnp.exp(scores - highest_score), -1, keepdims=True)))
        probability_reduced = low(jnp.exp(scores - log_total))
        return jnp.einsum('gcl,ld->cgd', probability_reduced, value_portion, precision=highest)
    result = lax.map(jax.checkpoint(one_head), (query_heads, key_heads, value_heads))
    return result.transpose(1, 0, 2, 3).reshape(seq_length, HEADS * HEAD_DIM)

def layer(seq_in, query_weight, key_weight, value_weight, output_weight, attn_gain, gate_weight, up_weight, down_weight, mlp_gain):
    seq_length = seq_in.shape[0]
    recip_one = lax.rsqrt(lax.optimization_barrier(jnp.mean(seq_in * seq_in, -1, keepdims=True)) + epsilon)
    normed_one = low(seq_in * recip_one * attn_gain)
    query_raw = low_back(product(normed_one, query_weight))
    key_raw = low_back(product(normed_one, key_weight))
    values_low = low(low_back(product(normed_one, value_weight)))
    cosine, sine_table = angles(seq_length, 0, HEAD_DIM)
    queries = low(rotate(query_raw, cosine, sine_table, HEAD_DIM) * HEAD_DIM ** (-0.5))
    keys_rot = low(rotate(key_raw, cosine, sine_table, HEAD_DIM))
    attended = low(low_back(attend(queries, keys_rot, values_low)))
    residual = seq_in + low_back(product(attended, output_weight))
    recip_two = lax.rsqrt(lax.optimization_barrier(jnp.mean(residual * residual, -1, keepdims=True)) + epsilon)
    normed_two = low(residual * recip_two * mlp_gain)
    gate_act = low_back(product(normed_two, gate_weight))
    up_act = low_back(product(normed_two, up_weight))
    hidden_low = low(jax.nn.silu(gate_act) * up_act)
    return residual + low_back(product(hidden_low, down_weight))

def reference(inputs, cotangent, query_weight, key_weight, value_weight, output_weight, attn_gain, gate_weight, up_weight, down_weight, mlp_gain):
    params = tuple((weight.astype(jnp.float32) for weight in (query_weight, key_weight, value_weight, output_weight, attn_gain, gate_weight, up_weight, down_weight, mlp_gain)))

    def one_sequence(totals, pair):
        seq_in, seq_grad = pair
        result, backward = jax.vjp(layer, seq_in.astype(jnp.float32), *params)
        grads = backward(seq_grad.astype(jnp.float32))
        totals = tuple((total + grad for total, grad in zip(totals, grads[1:])))
        return (totals, (result.astype(jnp.bfloat16), grads[0].astype(jnp.bfloat16)))
    starting = tuple((jnp.zeros_like(weight) for weight in params))
    totals, (layer_out, inputs_grad) = lax.scan(one_sequence, starting, (inputs, cotangent))
    return (layer_out, inputs_grad, totals[0], totals[1], totals[2], totals[3], totals[4], totals[5], totals[6], totals[7], totals[8])
```

```python
import functools

import jax
import jax.numpy as jnp
from jax import lax
from jax.sharding import PartitionSpec as P

HEADS = 16
KV_HEADS = 8
HEAD_DIM = 96


epsilon = 1e-05
rope_base = 100000.0


def angles(row_count, start_pos, head_dim):
    half_dim = head_dim // 2
    positions = (start_pos + jnp.arange(row_count, dtype=jnp.int32)).astype(jnp.float32)
    frequency = rope_base ** (-(2.0 * jnp.arange(half_dim, dtype=jnp.float32)) / head_dim)
    angle_table = positions[:, None] * frequency[None, :]
    return (jnp.cos(angle_table), jnp.sin(angle_table))


def rotate(field, cosine, sine_table, head_dim, inverse):
    field_shape = field.shape
    split_heads = field.reshape(field_shape[:-1] + (field_shape[-1] // head_dim, head_dim))
    half_dim = head_dim // 2
    first_half = split_heads[..., :half_dim]
    second_half = split_heads[..., half_dim:]
    cos_part = cosine[:, None, :]
    sin_part = sine_table[:, None, :]
    if inverse:
        rotated = jnp.concatenate(
            [
                first_half * cos_part + second_half * sin_part,
                second_half * cos_part - first_half * sin_part,
            ],
            -1,
        )
    else:
        rotated = jnp.concatenate(
            [
                first_half * cos_part - second_half * sin_part,
                second_half * cos_part + first_half * sin_part,
            ],
            -1,
        )
    return rotated.reshape(field_shape)


def body(
    inputs,
    cotangent,
    query_weight,
    key_weight,
    value_weight,
    output_weight,
    attn_gain,
    gate_weight,
    up_weight,
    down_weight,
    mlp_gain,
):
    seq_here, span_rows, model_width = inputs.shape
    token_rows = seq_here * span_rows
    ctx_rank = lax.axis_index("ctx")
    kv_width = KV_HEADS * HEAD_DIM
    group_size = HEADS // KV_HEADS
    group_width = group_size * HEAD_DIM
    score_scale = HEAD_DIM ** (-0.5)
    attn_full = (
        lax.all_gather(query_weight, ("dp", "ctx"), axis=0, tiled=True),
        lax.all_gather(key_weight, ("dp", "ctx"), axis=0, tiled=True),
        lax.all_gather(value_weight, ("dp", "ctx"), axis=0, tiled=True),
        lax.all_gather(output_weight, ("dp", "ctx"), axis=0, tiled=True),
        lax.all_gather(attn_gain, ("dp", "ctx"), axis=0, tiled=True),
    )
    query_full, key_full, value_full, output_full, attn_gain_full = attn_full
    input_widened = inputs.astype(jnp.float32).reshape(token_rows, model_width)
    recip_one = lax.rsqrt(jnp.mean(input_widened * input_widened, -1, keepdims=True) + epsilon)
    normed_one = (input_widened * recip_one * attn_gain_full.astype(jnp.float32)).astype(
        jnp.bfloat16
    )
    query_raw = jnp.dot(normed_one, query_full, preferred_element_type=jnp.float32)
    key_raw = jnp.dot(normed_one, key_full, preferred_element_type=jnp.float32)
    value_raw = jnp.dot(normed_one, value_full, preferred_element_type=jnp.float32)
    cosine, sine_table = angles(span_rows, ctx_rank * span_rows, HEAD_DIM)
    queries = (
        rotate(query_raw.reshape(seq_here, span_rows, -1), cosine, sine_table, HEAD_DIM, False)
        * score_scale
    ).astype(jnp.bfloat16)
    keys_rot = rotate(
        key_raw.reshape(seq_here, span_rows, -1), cosine, sine_table, HEAD_DIM, False
    ).astype(jnp.bfloat16)
    values_low = value_raw.reshape(seq_here, span_rows, kv_width).astype(jnp.bfloat16)
    kv_local = jnp.concatenate([keys_rot, values_low], -1)
    kv_all = lax.all_gather(kv_local, "ctx", axis=1, tiled=True)
    seq_length = kv_all.shape[1]
    query_place = ctx_rank * span_rows + jnp.arange(span_rows, dtype=jnp.int32)
    key_place = jnp.arange(seq_length, dtype=jnp.int32)
    allowed = key_place[None, :] <= query_place[:, None]

    def group_slice(source, kv_head):
        piece = lax.dynamic_slice_in_dim(source, kv_head * group_width, group_width, 2)
        return piece.reshape(seq_here, span_rows, group_size, HEAD_DIM)

    def head_parts(kv_source, kv_head):
        key_portion = lax.dynamic_slice_in_dim(kv_source, kv_head * HEAD_DIM, HEAD_DIM, 2)
        value_portion = lax.dynamic_slice_in_dim(
            kv_source, kv_width + kv_head * HEAD_DIM, HEAD_DIM, 2
        )
        return (key_portion, value_portion)

    def masked_scores(query_portion, key_portion):
        scores = jnp.einsum(
            "awuh,afh->auwf", query_portion, key_portion, preferred_element_type=jnp.float32
        )
        return jnp.where(allowed[None, None], scores, -1e30)

    def forward_head(attended, kv_head):
        query_portion = group_slice(queries, kv_head)
        key_portion, value_portion = head_parts(kv_all, kv_head)
        scores = masked_scores(query_portion, key_portion)
        highest_score = jnp.max(scores, -1, keepdims=True)
        log_total = highest_score + jnp.log(
            jnp.sum(jnp.exp(scores - highest_score), -1, keepdims=True)
        )
        probability_reduced = jnp.exp(scores - log_total).astype(jnp.bfloat16)
        head_out = jnp.einsum(
            "obzf,ofp->ozbp", probability_reduced, value_portion, preferred_element_type=jnp.float32
        )
        attended = lax.dynamic_update_slice_in_dim(
            attended, head_out.reshape(seq_here, span_rows, group_width), kv_head * group_width, 2
        )
        return (attended, log_total)

    head_ids = jnp.arange(KV_HEADS, dtype=jnp.int32)
    attended_work, log_totals = lax.scan(
        forward_head, jnp.zeros((seq_here, span_rows, HEADS * HEAD_DIM), jnp.float32), head_ids
    )
    attended_work_low = attended_work.astype(jnp.bfloat16)
    attended_low = attended_work_low.reshape(token_rows, -1)
    residual = input_widened + jnp.dot(
        attended_low, output_full, preferred_element_type=jnp.float32
    )
    mlp_full = (
        lax.all_gather(gate_weight, ("dp", "ctx"), axis=0, tiled=True),
        lax.all_gather(up_weight, ("dp", "ctx"), axis=0, tiled=True),
        lax.all_gather(down_weight, ("dp", "ctx"), axis=0, tiled=True),
        lax.all_gather(mlp_gain, ("dp", "ctx"), axis=0, tiled=True),
    )
    gate_full, up_full, down_full, mlp_gain_full = mlp_full
    recip_two = lax.rsqrt(jnp.mean(residual * residual, -1, keepdims=True) + epsilon)
    normed_two = (residual * recip_two * mlp_gain_full.astype(jnp.float32)).astype(jnp.bfloat16)
    gate_act = jnp.dot(normed_two, gate_full, preferred_element_type=jnp.float32)
    up_act = jnp.dot(normed_two, up_full, preferred_element_type=jnp.float32)
    sigmoid_gate = jax.nn.sigmoid(gate_act)
    silu_gate = gate_act * sigmoid_gate
    hidden_low = (silu_gate * up_act).astype(jnp.bfloat16)
    layer_out = (
        (residual + jnp.dot(hidden_low, down_full, preferred_element_type=jnp.float32))
        .astype(jnp.bfloat16)
        .reshape(inputs.shape)
    )
    back_mlp = (
        lax.all_gather(gate_weight, ("dp", "ctx"), axis=0, tiled=True),
        lax.all_gather(up_weight, ("dp", "ctx"), axis=0, tiled=True),
        lax.all_gather(down_weight, ("dp", "ctx"), axis=0, tiled=True),
        lax.all_gather(mlp_gain, ("dp", "ctx"), axis=0, tiled=True),
    )
    back_attn = (
        lax.all_gather(query_weight, ("dp", "ctx"), axis=0, tiled=True),
        lax.all_gather(key_weight, ("dp", "ctx"), axis=0, tiled=True),
        lax.all_gather(value_weight, ("dp", "ctx"), axis=0, tiled=True),
        lax.all_gather(output_weight, ("dp", "ctx"), axis=0, tiled=True),
        lax.all_gather(attn_gain, ("dp", "ctx"), axis=0, tiled=True),
    )
    gate_back, up_back, down_back, mlp_gain_back = back_mlp
    query_back, key_back, value_back, output_back, attn_gain_back = back_attn
    grad_out = cotangent.reshape(token_rows, model_width)
    grad_hidden = jnp.einsum("nd,fd->nf", grad_out, down_back, preferred_element_type=jnp.float32)
    grad_gate = (
        grad_hidden * up_act * sigmoid_gate * (1.0 + gate_act * (1.0 - sigmoid_gate))
    ).astype(jnp.bfloat16)
    grad_up = (grad_hidden * silu_gate).astype(jnp.bfloat16)
    grad_two = jnp.einsum(
        "nf,df->nd", grad_gate, gate_back, preferred_element_type=jnp.float32
    ) + jnp.einsum("nf,df->nd", grad_up, up_back, preferred_element_type=jnp.float32)
    scaled_two = grad_two * mlp_gain_back.astype(jnp.float32)
    mlp_gain_term = jnp.sum(grad_two * residual * recip_two, 0)
    grad_residual = (
        grad_out.astype(jnp.float32)
        + recip_two * scaled_two
        - residual * recip_two**3 * jnp.mean(scaled_two * residual, -1, keepdims=True)
    )
    down_grad = lax.psum_scatter(
        jnp.einsum("nf,nd->fd", hidden_low, grad_out, preferred_element_type=jnp.float32),
        ("dp", "ctx"),
        scatter_dimension=0,
        tiled=True,
    )
    grad_branch = grad_residual.astype(jnp.bfloat16)
    grad_attended = (
        jnp.einsum("nd,kd->nk", grad_branch, output_back, preferred_element_type=jnp.float32)
        .astype(jnp.bfloat16)
        .reshape(seq_here, span_rows, -1)
    )
    kv_back = lax.all_gather(kv_local, "ctx", axis=1, tiled=True)

    def backward_head(carry, head_pair):
        grad_queries, grad_kv = carry
        kv_head, log_total = head_pair
        query_portion = group_slice(queries, kv_head)
        gradient_portion = group_slice(grad_attended, kv_head)
        key_portion, value_portion = head_parts(kv_back, kv_head)
        scores = masked_scores(query_portion, key_portion)
        probs = jnp.exp(scores - log_total)
        probability_reduced = probs.astype(jnp.bfloat16)
        grad_probs = jnp.einsum(
            "awuh,afh->auwf", gradient_portion, value_portion, preferred_element_type=jnp.float32
        )
        weighted = jnp.sum(probs * grad_probs, -1, keepdims=True)
        score_gradient = (probs * (grad_probs - weighted)).astype(jnp.bfloat16)
        query_fragment = jnp.einsum(
            "obzf,ofp->ozbp", score_gradient, key_portion, preferred_element_type=jnp.float32
        )
        key_piece = jnp.einsum(
            "abfq,afbi->aqi", score_gradient, query_portion, preferred_element_type=jnp.float32
        )
        value_piece = jnp.einsum(
            "abfq,afbi->aqi",
            probability_reduced,
            gradient_portion,
            preferred_element_type=jnp.float32,
        )
        grad_queries = lax.dynamic_update_slice_in_dim(
            grad_queries,
            query_fragment.reshape(seq_here, span_rows, group_width),
            kv_head * group_width,
            2,
        )
        grad_kv = lax.dynamic_update_slice_in_dim(grad_kv, key_piece, kv_head * HEAD_DIM, 2)
        grad_kv = lax.dynamic_update_slice_in_dim(
            grad_kv, value_piece, kv_width + kv_head * HEAD_DIM, 2
        )
        return ((grad_queries, grad_kv), None)

    start_carry = (
        jnp.zeros((seq_here, span_rows, HEADS * HEAD_DIM), jnp.float32),
        jnp.zeros((seq_here, seq_length, 2 * kv_width), jnp.float32),
    )
    (grad_queries_work, grad_kv), unused = lax.scan(
        backward_head, start_carry, (head_ids, log_totals)
    )
    grad_queries = grad_queries_work
    kv_grad = lax.psum_scatter(grad_kv, "ctx", scatter_dimension=1, tiled=True)
    grad_q = (
        rotate(grad_queries * score_scale, cosine, sine_table, HEAD_DIM, True)
        .astype(jnp.bfloat16)
        .reshape(token_rows, -1)
    )
    grad_k = (
        rotate(kv_grad[..., :kv_width], cosine, sine_table, HEAD_DIM, True)
        .astype(jnp.bfloat16)
        .reshape(token_rows, -1)
    )
    grad_v = kv_grad[..., kv_width:].astype(jnp.bfloat16).reshape(token_rows, -1)
    grad_one = jnp.einsum("nk,dk->nd", grad_q, query_back, preferred_element_type=jnp.float32)
    grad_one = grad_one + jnp.einsum(
        "nk,dk->nd", grad_k, key_back, preferred_element_type=jnp.float32
    )
    grad_one = grad_one + jnp.einsum(
        "nk,dk->nd", grad_v, value_back, preferred_element_type=jnp.float32
    )
    scaled_one = grad_one * attn_gain_back.astype(jnp.float32)
    attn_gain_term = jnp.sum(grad_one * input_widened * recip_one, 0)
    inputs_grad = (
        (
            grad_residual
            + recip_one * scaled_one
            - input_widened * recip_one**3 * jnp.mean(scaled_one * input_widened, -1, keepdims=True)
        )
        .astype(jnp.bfloat16)
        .reshape(inputs.shape)
    )
    grad_projected = jnp.concatenate([grad_q, grad_k, grad_v], -1)
    grad_mlp_in = jnp.concatenate([grad_gate, grad_up], -1)
    projected_term = jnp.einsum(
        "nd,nk->dk", normed_one, grad_projected, preferred_element_type=jnp.float32
    )
    output_term = jnp.einsum(
        "nk,nd->kd", attended_low, grad_branch, preferred_element_type=jnp.float32
    )
    mlp_term = jnp.einsum("nd,nf->df", normed_two, grad_mlp_in, preferred_element_type=jnp.float32)
    row_grad = lax.psum_scatter(
        jnp.concatenate([projected_term, output_term, mlp_term], 1),
        ("dp", "ctx"),
        scatter_dimension=0,
        tiled=True,
    )
    gain_grad = lax.psum_scatter(
        jnp.stack([attn_gain_term, mlp_gain_term]), ("dp", "ctx"), scatter_dimension=1, tiled=True
    )
    q_width = HEADS * HEAD_DIM
    value_start = q_width + kv_width
    output_start = value_start + kv_width
    gate_start = output_start + model_width
    ff_width = gate_back.shape[1]
    up_start = gate_start + ff_width
    query_grad = row_grad[:, :q_width]
    key_grad = row_grad[:, q_width:value_start]
    value_grad = row_grad[:, value_start:output_start]
    output_grad = row_grad[:, output_start:gate_start]
    gate_grad = row_grad[:, gate_start:up_start]
    up_grad = row_grad[:, up_start : up_start + ff_width]
    return (
        layer_out,
        inputs_grad,
        query_grad,
        key_grad,
        value_grad,
        output_grad,
        gain_grad[0],
        gate_grad,
        up_grad,
        down_grad,
        gain_grad[1],
    )


def row_norm(field):
    return lax.rsqrt(jnp.mean(field * field, -1, keepdims=True) + epsilon)


def gather_ctx(block):
    return lax.all_gather(block, "ctx", axis=1, tiled=True)


def reduce_ctx(partial):
    return lax.psum_scatter(partial, "ctx", scatter_dimension=1, tiled=True)


def mm(left, right, dims):
    return jnp.einsum(dims, left, right, preferred_element_type=jnp.float32)


def head_body(
    dp_size,
    inputs,
    cotangent,
    query_weight,
    key_weight,
    value_weight,
    output_weight,
    attn_gain,
    gate_weight,
    up_weight,
    down_weight,
    mlp_gain,
):
    f32, bf16 = jnp.float32, jnp.bfloat16
    ranks = KV_HEADS
    seq_here, span_rows, model_width = inputs.shape
    seq_length = span_rows * ranks
    tokens = seq_here * seq_length
    local = seq_here * span_rows
    weight_rows = query_weight.shape[0]
    ff_width = gate_weight.shape[1]
    group = HEADS // KV_HEADS
    group_width = group * HEAD_DIM
    head_width = group_width + 2 * HEAD_DIM
    piece = down_weight.shape[0]
    hidden_width = dp_size * piece
    score_scale = HEAD_DIM ** (-0.5)

    def columns(weight, width):
        return weight.reshape(weight_rows, ranks, width)

    def hidden_columns(weight):
        split = weight.reshape(weight_rows, dp_size, ranks, piece)
        return split.transpose(2, 0, 1, 3).reshape(ranks, weight_rows, hidden_width)

    def exchange(packed):
        return lax.all_to_all(packed, "ctx", split_axis=0, concat_axis=0, tiled=True)

    head_pack = jnp.concatenate(
        [
            columns(query_weight, group_width),
            columns(key_weight, HEAD_DIM),
            columns(value_weight, HEAD_DIM),
        ],
        -1,
    ).transpose(1, 0, 2)
    head_mine = exchange(head_pack).reshape(ranks * weight_rows, head_width)
    head_weight = lax.all_gather(head_mine, "dp", axis=0, tiled=True)
    shards = dp_size * ranks
    to_rank = [(i, ranks * (i % dp_size) + i // dp_size) for i in range(shards)]
    from_rank = [(b, a) for a, b in to_rank]
    out_mine = lax.ppermute(output_weight, ("dp", "ctx"), to_rank)
    out_weight = lax.all_gather(out_mine, "dp", axis=0, tiled=True)
    mlp_pack = jnp.concatenate([hidden_columns(gate_weight), hidden_columns(up_weight)], -1)
    mlp_mine = exchange(mlp_pack).reshape(ranks * weight_rows, 2 * hidden_width)
    mlp_weight = lax.all_gather(mlp_mine, "dp", axis=0, tiled=True)
    down_full = lax.all_gather(down_weight, "dp", axis=0, tiled=True)
    gains = lax.all_gather(jnp.stack([attn_gain, mlp_gain]), ("dp", "ctx"), axis=1, tiled=True)
    attn_gain_full = gains[0].astype(f32)
    mlp_gain_full = gains[1].astype(f32)

    field = gather_ctx(inputs).astype(f32).reshape(tokens, model_width)
    normed_one = (field * row_norm(field) * attn_gain_full).astype(bf16)
    heads_raw = mm(normed_one, head_weight, "nd,dk->nk").reshape(seq_here, seq_length, head_width)
    cosine, sine_table = angles(seq_length, 0, HEAD_DIM)
    queries = (
        rotate(heads_raw[..., :group_width], cosine, sine_table, HEAD_DIM, False) * score_scale
    ).astype(bf16)
    keys_rot = rotate(
        heads_raw[..., group_width : group_width + HEAD_DIM], cosine, sine_table, HEAD_DIM, False
    ).astype(bf16)
    values_low = heads_raw[..., group_width + HEAD_DIM :].astype(bf16)
    queries = queries.reshape(seq_here, seq_length, group, HEAD_DIM)
    place = jnp.arange(seq_length, dtype=jnp.int32)
    allowed = (place[None, :] <= place[:, None])[None, None]
    scores = jnp.where(allowed, mm(queries, keys_rot, "sqgd,skd->sgqk"), -1e30)
    highest_score = jnp.max(scores, -1, keepdims=True)
    log_total = highest_score + jnp.log(
        jnp.sum(jnp.exp(scores - highest_score), -1, keepdims=True)
    )
    probs = jnp.exp(scores - log_total)
    probs_low = probs.astype(bf16)
    attended = mm(probs_low, values_low, "sgqk,skd->sqgd").astype(bf16)
    attended = attended.reshape(tokens, group_width)
    branch = mm(attended, out_weight, "nk,kd->nd").astype(bf16)
    branch = reduce_ctx(branch.reshape(seq_here, seq_length, model_width))
    own = inputs.astype(f32).reshape(local, model_width)
    residual = own + branch.astype(f32).reshape(local, model_width)
    recip_two = row_norm(residual)
    normed_two = (residual * recip_two * mlp_gain_full).astype(bf16)
    normed_all = gather_ctx(normed_two.reshape(inputs.shape)).reshape(tokens, model_width)
    both = mm(normed_all, mlp_weight, "nd,df->nf")
    gate_act = both[:, :hidden_width]
    up_act = both[:, hidden_width:]
    sigmoid_gate = jax.nn.sigmoid(gate_act)
    silu_gate = gate_act * sigmoid_gate
    hidden_low = (silu_gate * up_act).astype(bf16)
    mlp_out = mm(hidden_low, down_full, "nf,fd->nd").astype(bf16)
    mlp_out = reduce_ctx(mlp_out.reshape(seq_here, seq_length, model_width))
    layer_out = (residual + mlp_out.astype(f32).reshape(local, model_width)).astype(bf16)

    grad_all = gather_ctx(cotangent).reshape(tokens, model_width)
    grad_hidden = mm(grad_all, down_full, "nd,fd->nf")
    grad_gate = (
        grad_hidden * up_act * sigmoid_gate * (1.0 + gate_act * (1.0 - sigmoid_gate))
    ).astype(bf16)
    grad_up = (grad_hidden * silu_gate).astype(bf16)
    grad_both = jnp.concatenate([grad_gate, grad_up], -1)
    grad_two = mm(grad_both, mlp_weight, "nf,df->nd").astype(bf16)
    grad_two = reduce_ctx(grad_two.reshape(seq_here, seq_length, model_width))
    grad_two = grad_two.astype(f32).reshape(local, model_width)
    scaled_two = grad_two * mlp_gain_full
    grad_own = cotangent.astype(f32).reshape(local, model_width)
    grad_residual = (
        grad_own
        + recip_two * scaled_two
        - residual * recip_two**3 * jnp.mean(scaled_two * residual, -1, keepdims=True)
    )
    grad_branch = grad_residual.astype(bf16).reshape(inputs.shape)
    branch_all = gather_ctx(grad_branch).reshape(tokens, model_width)

    def reduce_dp(partial):
        return lax.psum_scatter(partial.astype(bf16), "dp", scatter_dimension=0, tiled=True)

    def back_exchange(rows):
        return exchange(rows.reshape(ranks, weight_rows, -1)).astype(f32)

    down_grad = reduce_dp(mm(hidden_low, grad_all, "nf,nd->fd")).astype(f32)
    mlp_grad = back_exchange(reduce_dp(mm(normed_all, grad_both, "nd,nf->df")))

    def hidden_rows(block):
        split = block.reshape(ranks, weight_rows, dp_size, piece)
        return split.transpose(1, 2, 0, 3).reshape(weight_rows, ff_width)

    gate_grad = hidden_rows(mlp_grad[..., :hidden_width])
    up_grad = hidden_rows(mlp_grad[..., hidden_width:])

    grad_attended = mm(branch_all, out_weight, "nd,kd->nk").astype(bf16)
    out_partial = reduce_dp(mm(attended, branch_all, "nk,nd->kd"))
    output_grad = lax.ppermute(out_partial, ("dp", "ctx"), from_rank).astype(f32)
    grad_heads = grad_attended.reshape(seq_here, seq_length, group, HEAD_DIM)
    grad_probs = mm(grad_heads, values_low, "sqgd,skd->sgqk")
    weighted = jnp.sum(probs * grad_probs, -1, keepdims=True)
    grad_scores = (probs * (grad_probs - weighted)).astype(bf16)
    grad_queries = mm(grad_scores, keys_rot, "sgqk,skd->sqgd").reshape(
        seq_here, seq_length, group_width
    )
    grad_keys = mm(grad_scores, queries, "sgqk,sqgd->skd")
    grad_values = mm(probs_low, grad_heads, "sgqk,sqgd->skd")
    grad_q = rotate(grad_queries * score_scale, cosine, sine_table, HEAD_DIM, True)
    grad_k = rotate(grad_keys, cosine, sine_table, HEAD_DIM, True)
    grad_project = jnp.concatenate([grad_q, grad_k, grad_values], -1).astype(bf16)
    grad_project = grad_project.reshape(tokens, head_width)
    grad_one = mm(grad_project, head_weight, "nk,dk->nd").astype(bf16)
    grad_one = reduce_ctx(grad_one.reshape(seq_here, seq_length, model_width))
    grad_one = grad_one.astype(f32).reshape(local, model_width)
    head_grad = back_exchange(reduce_dp(mm(normed_one, grad_project, "nd,nk->dk")))
    recip_one = row_norm(own)
    scaled_one = grad_one * attn_gain_full
    inputs_grad = (
        grad_residual
        + recip_one * scaled_one
        - own * recip_one**3 * jnp.mean(scaled_one * own, -1, keepdims=True)
    ).astype(bf16)

    def from_heads(block):
        return block.transpose(1, 0, 2).reshape(weight_rows, -1)

    query_grad = from_heads(head_grad[..., :group_width])
    key_grad = from_heads(head_grad[..., group_width : group_width + HEAD_DIM])
    value_grad = from_heads(head_grad[..., group_width + HEAD_DIM :])

    def overlap(weight, grad):
        return jnp.sum(weight.astype(f32) * grad, -1)

    attn_gain_grad = (
        overlap(query_weight, query_grad)
        + overlap(key_weight, key_grad)
        + overlap(value_weight, value_grad)
    ) / attn_gain.astype(f32)
    mlp_gain_grad = (overlap(gate_weight, gate_grad) + overlap(up_weight, up_grad)) / (
        mlp_gain.astype(f32)
    )
    return (
        layer_out.reshape(inputs.shape),
        inputs_grad.reshape(inputs.shape),
        query_grad,
        key_grad,
        value_grad,
        output_grad,
        attn_gain_grad,
        gate_grad,
        up_grad,
        down_grad,
        mlp_gain_grad,
    )


def solution(mesh):
    placed = (
        P("dp", "ctx", None),
        P("dp", "ctx", None),
        P(("dp", "ctx"), None),
        P(("dp", "ctx"), None),
        P(("dp", "ctx"), None),
        P(("dp", "ctx"), None),
        P(("dp", "ctx")),
        P(("dp", "ctx"), None),
        P(("dp", "ctx"), None),
        P(("dp", "ctx"), None),
        P(("dp", "ctx")),
    )
    dp_size, ctx_size = mesh.shape["dp"], mesh.shape["ctx"]
    chosen = functools.partial(head_body, dp_size) if ctx_size == KV_HEADS else body
    return jax.shard_map(
        chosen,
        mesh=mesh,
        in_specs=placed,
        out_specs=(
            P("dp", "ctx", None),
            P("dp", "ctx", None),
            P(("dp", "ctx"), None),
            P(("dp", "ctx"), None),
            P(("dp", "ctx"), None),
            P(("dp", "ctx"), None),
            P(("dp", "ctx")),
            P(("dp", "ctx"), None),
            P(("dp", "ctx"), None),
            P(("dp", "ctx"), None),
            P(("dp", "ctx")),
        ),
        check_vma=False,
    )
```
